512 devices in a mesh: row: 16 (over y, core), col: 16 (over z_hi, x), smp: 2 (over z_lo).
Axes of the slice: x: 4, y: 8, z: 8 (z_hi: 4, z_lo: 2; z = z_hi * 2 + z_lo), core: 2. Of those that a mesh axis runs over, the one named last changes fastest.
Arguments:
- precision: float32 [8192, 8192], P('row', 'col'), as said below
- residuals: float32 [8192, 1024], P(('col', 'row'), 'smp'), may hold values from -6 to 6
- labels: int32 [8192], replicated, may hold values from 0 to 3
Outputs:
- updated: float32 [8192, 8192], P('row', 'col')
The draws below stay inside these ranges and needn't reach their ends.
Inputs may be any that keep to these rules, and one draw needn't show every extreme that they name: `precision`: symmetric; diagonal entries from 1.5 to 3.
All inputs are finite; a program needn't handle non-finite values.
Results may differ from the reference program's by a relative error of at most 0.0003.
Values sent between devices are 32-bit elements; how exact they have to be, the bound alone decides.
A program may use at most 64 MiB of HBM per device.

```python
import jax
import jax.numpy as jnp
from jax import lax

COMPS = 4
SERIES = 8192
SAMPLES = 1024


def draw_precision(key, part):
    first, second = jax.random.split(jax.random.fold_in(key, 17), 2)
    base = jax.random.normal(first, (SERIES, SERIES), jnp.float32) * (0.5 / SERIES ** 0.5)
    offdiag = (base + base.T) * 0.5 ** 0.5
    diag = jax.random.uniform(second, (SERIES,), jnp.float32, 1.5, 3.0)
    ident = jnp.eye(SERIES, dtype=jnp.float32)
    return offdiag * (1.0 - ident) + ident * diag[:, None]


def plant(drawn, rng, least, high):
    longest = drawn.shape.index(max(drawn.shape))
    spots = []
    for shift in (0, 1):
        where = [jax.random.randint(jax.random.fold_in(rng, axis), (), 0, length) for axis, length in enumerate(drawn.shape)]
        where[longest] = (where[longest] + shift) % drawn.shape[longest]
        spots.append(tuple(where))
    return drawn.at[spots[0]].set(least).at[spots[1]].set(high)


def level_of(stream_key, shape, cuts, smallest, top_value):
    factor_of, own = 1.0, jax.random.fold_in(stream_key, 6)
    for axis_at, parts in cuts:
        heights = jnp.exp(jax.random.uniform(jax.random.fold_in(own, axis_at), (parts,), jnp.float32, smallest / len(cuts), top_value / len(cuts)))
        factor_of = factor_of * jnp.repeat(heights, shape[axis_at] // parts).reshape([-1 if axis == axis_at else 1 for axis in range(len(shape))])
    return factor_of


def bell_draw(stream_key, shape, deviation, most, shards=(), held_as=jnp.bfloat16):
    level = level_of(stream_key, shape, shards, -0.22, 0.18) if shards else 1.0
    array = jax.random.normal(stream_key, shape, jnp.float32) * deviation * level
    return jnp.minimum(jnp.maximum(array, -most), most).astype(held_as)


def setup_inputs(seed: int = 0) -> dict:
    seeds = jax.random.split(jax.random.key(seed), 4)
    precision = draw_precision(jax.random.fold_in(seeds[3], 71), 0)
    residuals = bell_draw(seeds[1], (SERIES, SAMPLES), 1.0, 6.0, ((0, 256), (1, 2)), jnp.float32)
    labels = plant(jax.random.randint(seeds[2], (SERIES,), 0, COMPS), jax.random.fold_in(seeds[2], 1), 0, COMPS - 1).astype(jnp.int32)
    return {"precision": precision, "residuals": residuals, "labels": labels}


STEP_SIZE = 0.5
PENALTY = 0.04


def reference(precision, residuals, labels):
    image = jnp.dot(precision, residuals, precision=lax.Precision.HIGHEST, preferred_element_type=jnp.float32)
    gram = jnp.dot(image, residuals.T, precision=lax.Precision.HIGHEST, preferred_element_type=jnp.float32)
    count = residuals.shape[1]
    ident = jnp.eye(precision.shape[0], dtype=jnp.float32)
    diag = jnp.diagonal(precision)
    gradient = (gram + gram.T) / (2.0 * count) - ident * (1.0 / diag)[:, None]
    moved = precision - STEP_SIZE * gradient
    shrunk = jnp.sign(moved) * jnp.maximum(jnp.abs(moved) - STEP_SIZE * PENALTY, 0.0)
    same = (labels[:, None] == labels[None, :]).astype(jnp.float32)
    return ident * moved + (1.0 - ident) * shrunk * same
```

```python
import heapq

import jax
import jax.numpy as jnp
from jax import lax
from jax.experimental import pallas as pl
from jax.experimental.pallas import tpu as pltpu
from jax.sharding import PartitionSpec as P

STEP_SIZE = 0.5
PENALTY = 0.04
NY, NX, NZ = 8, 4, 4
SEMS = 160
MESH = pl.DeviceIdType.MESH
F32, BF16 = jnp.float32, jnp.bfloat16


def split(a):
    high = a.astype(BF16)
    return high, (a - high.astype(F32)).astype(BF16)


def product(a, b, dims):
    (ah, al), (bh, bl) = a, b

    def dot(p, q):
        return lax.dot_general(p, q, (dims, ((), ())), preferred_element_type=F32)

    return dot(ah, bh) + dot(ah, bl) + dot(al, bh)


def kernel(count, om, x, lab, out, XJ, WJ, WI, XI, PT, RX, RC, S, RZ, ZC, OM, SAME, XH, XL, WH, WL, ssem, rsem, lsem):
    row, col, u = lax.axis_index("row"), lax.axis_index("col"), lax.axis_index("smp")
    y, core = row // 2, row % 2
    zh, xx = col // NX, col % NX
    v = 1 - u

    def ring(at, by, size):
        return lax.rem(at + by + size, size)

    up, down = {"row": ring(y, 1, NY) * 2 + core}, {"row": ring(y, -1, NY) * 2 + core}
    mate = {"row": y * 2 + 1 - core}
    east, west = {"col": zh * NX + ring(xx, 1, NX)}, {"col": zh * NX + ring(xx, -1, NX)}
    north, south = {"col": ring(zh, 1, NZ) * NX + xx}, {"col": ring(zh, -1, NZ) * NX + xx}
    peer = {"smp": v}
    mirror = {"row": col, "col": row}
    on_diagonal = row == col

    ids = {}
    sent = []

    def tag(key):
        return ids.setdefault(key, len(ids))

    def describe(key, src, dst, to):
        t = tag(key)
        return pltpu.make_async_remote_copy(
            src_ref=src, dst_ref=dst, send_sem=ssem.at[t], recv_sem=rsem.at[t], device_id=to, device_id_type=MESH
        )

    def send(key, src, dst, to):
        copy = describe(key, src, dst, to)
        copy.start()
        sent.append(copy)

    def take(key, dst, to):
        describe(key, dst, dst, to).wait_recv()

    load_x = pltpu.make_async_copy(x, XJ.at[y, core, u], lsem.at[0])
    load_om = pltpu.make_async_copy(om.at[:, :, u], OM, lsem.at[1])
    load_x.start()
    load_om.start()

    barrier = pltpu.get_barrier_semaphore()
    near = (up, down, mate, east, west, north, south, peer)
    for other in near:
        pl.semaphore_signal(barrier, inc=1, device_id=other, device_id_type=MESH)
    pl.semaphore_wait(barrier, len(near))
    load_x.wait()

    def to_mate(name, key, block):
        t = tag((name, "mate", key))
        copy = pltpu.make_async_remote_copy(
            src_ref=block, dst_ref=block, send_sem=ssem.at[t], recv_sem=rsem.at[tag((name, "mate"))],
            device_id=mate, device_id_type=MESH,
        )
        copy.start()
        sent.append(copy)

    def gather_lines(name, B, start, pace):
        own = B.at[y, core, u]
        send((name, "z0"), own, own, peer)
        send((name, "up", 1), own, own, up)
        send((name, "down", 1), own, own, down)
        to_mate(name, "own", own)
        yield start + pace
        theirs = B.at[y, core, v]
        take((name, "z0"), theirs, peer)
        half = B.at[y, core, v, 0]
        send((name, "up v", 1), half, half, up)
        send((name, "down v", 1), half, half, down)
        to_mate(name, "own v", theirs)
        late = []

        def settle():
            for k, below in late:
                at = ring(y, -k if below else k, NY)
                quarter = B.at[at, core, v, 1]
                take((name, "z", k, below), quarter, peer)
                to_mate(name, ("z", k, below), quarter)
            late.clear()

        for k in range(1, NY // 2):
            yield start + pace * (k + 1)
            for below, way, back in ((True, up, down), (False, down, up)):
                verb = "up" if below else "down"
                block = B.at[ring(y, -k if below else k, NY), core, u]
                take((name, verb, k), block, back)
                if k < NY // 2 - 1:
                    send((name, verb, k + 1), block, block, way)
                else:
                    piece = block.at[0 if below else 1]
                    send((name, verb, k + 1), piece, piece, way)
                piece = block.at[1]
                send((name, "z", k, below), piece, piece, peer)
                to_mate(name, ("u", k, below), block)
            for below, way, back in ((True, up, down), (False, down, up)):
                verb = "up" if below else "down"
                block = B.at[ring(y, -k if below else k, NY), core, v, 0]
                take((name, verb + " v", k), block, back)
                if k < NY // 2 - 1:
                    send((name, verb + " v", k + 1), block, block, way)
                to_mate(name, ("v", k, below), block)
            settle()
            late.extend([(k, True), (k, False)])
        yield start + pace * (NY // 2 + 1)
        far = B.at[ring(y, NY // 2, NY), core, u]
        take((name, "up", NY // 2), far.at[0], down)
        take((name, "down", NY // 2), far.at[1], up)
        send((name, "z far"), far, far, peer)
        to_mate(name, "far", far)
        settle()
        yield start + pace * (NY // 2 + 2)
        far = B.at[ring(y, NY // 2, NY), core, v]
        take((name, "z far"), far, peer)
        to_mate(name, "far v", far)
        yield start + pace * (NY // 2 + 3)
        whole = B.at[:, 1 - core]
        pltpu.make_async_remote_copy(
            src_ref=whole, dst_ref=whole, send_sem=ssem.at[0], recv_sem=rsem.at[tag((name, "mate"))],
            device_id=mate, device_id_type=MESH,
        ).wait_recv()

    def gather_plane(name, B, start, pace):
        def spread(z_to, key):
            block = B.at[z_to, xx]
            send((name, "east", key), block, block, east)
            send((name, "west", key), block, block, west)

        def pass_on(z_to, key):
            block = B.at[z_to, ring(xx, -1, NX)]
            take((name, "east", key), block, west)
            send((name, "east 2", key), block.at[0], block.at[0], east)
            block = B.at[z_to, ring(xx, 1, NX)]
            take((name, "west", key), block, east)
            send((name, "west 2", key), block.at[1], block.at[1], west)

        own = B.at[zh, xx]
        send((name, "north"), own, own, north)
        send((name, "south"), own, own, south)
        spread(zh, 0)
        yield start + pace
        block = B.at[ring(zh, -1, NZ), xx]
        take((name, "north"), block, south)
        send((name, "north 2"), block.at[0], block.at[0], north)
        spread(ring(zh, -1, NZ), 1)
        block = B.at[ring(zh, 1, NZ), xx]
        take((name, "south"), block, north)
        send((name, "south 2"), block.at[1], block.at[1], south)
        spread(ring(zh, 1, NZ), 2)
        yield start + pace
        pass_on(zh, 0)
        yield start + pace * 2
        far = B.at[ring(zh, 2, NZ), xx]
        take((name, "north 2"), far.at[0], south)
        take((name, "south 2"), far.at[1], north)
        spread(ring(zh, 2, NZ), 3)
        yield start + pace * 2
        pass_on(ring(zh, -1, NZ), 1)
        yield start + pace * 2.5
        pass_on(ring(zh, 1, NZ), 2)
        yield start + pace * 3
        pass_on(ring(zh, 2, NZ), 3)

    def finish_plane(name, B):
        for key, by in ((0, 0), (1, -1), (2, 1), (3, 2)):
            block = B.at[ring(zh, by, NZ), ring(xx, 2, NX)]
            take((name, "east 2", key), block.at[0], west)
            take((name, "west 2", key), block.at[1], east)

    def run(*phases):
        heap = []
        for n, phase in enumerate(phases):
            heap.append((-1.0, n, phase))
        heapq.heapify(heap)
        while heap:
            _, n, phase = heapq.heappop(heap)
            when = next(phase, None)
            if when is not None:
                heapq.heappush(heap, (when, n, phase))

    phase = gather_lines("X", XJ, 0, 1)
    next(phase)
    classes = lax.broadcasted_iota(jnp.int32, (8, 512), 0)
    ones = (lab[row] == classes).astype(BF16), (lab[col] == classes).astype(BF16)
    same = lax.dot_general(ones[0], ones[1], (((0,), (0,)), ((), ())), preferred_element_type=F32)
    SAME[...] = same.reshape(SAME.shape)
    for _ in phase:
        pass

    load_om.wait()
    om_parts = split(OM[...].reshape(256, 512))
    x2 = ring(xx, 2, NX)
    xe, xw = ring(xx, 1, NX), ring(xx, -1, NX)
    z2 = ring(zh, 2, NZ)
    zn, zs = ring(zh, 1, NZ), ring(zh, -1, NZ)
    low, high = pl.ds(0, 2), pl.ds(2, 2)
    for q in range(2):
        x_parts = split(XJ[:, :, q].reshape(512, 512))
        XH[q], XL[q] = x_parts
        PT[:, :, q] = product(om_parts, x_parts, ((1,), (0,))).reshape(NZ, NX, 16, 512)
        send(("rs far e", q), PT.at[low, x2, q], RX.at[0, q], east)
        send(("rs far w", q), PT.at[high, x2, q], RX.at[1, q], west)
        send(("rs now e", q), PT.at[high, xe, q], RC.at[0, q, high], east)
        send(("rs now w", q), PT.at[low, xw, q], RC.at[1, q, low], west)
    for q in range(2):
        take(("rs far e", q), RX.at[0, q], west)
        PT[low, xe, q] += RX[0, q]
        send(("rs e", q), PT.at[low, xe, q], RC.at[0, q, low], east)
        take(("rs far w", q), RX.at[1, q], east)
        PT[high, xw, q] += RX[1, q]
        send(("rs w", q), PT.at[high, xw, q], RC.at[1, q, high], west)
    top, bottom = pl.ds(0, 8), pl.ds(8, 8)
    for q in range(2):
        take(("rs now e", q), RC.at[0, q, high], west)
        take(("rs now w", q), RC.at[1, q, low], east)
        take(("rs e", q), RC.at[0, q, low], west)
        take(("rs w", q), RC.at[1, q, high], east)
        S[q] = PT[:, xx, q] + RC[0, q] + RC[1, q]
        send(("rz far n", q), S.at[q, z2, top], RZ.at[0, q], north)
        send(("rz far s", q), S.at[q, z2, bottom], RZ.at[1, q], south)
        send(("rz now n", q), S.at[q, zn, bottom], ZC.at[0, q, bottom], north)
        send(("rz now s", q), S.at[q, zs, top], ZC.at[1, q, top], south)
    for q in range(2):
        take(("rz far n", q), RZ.at[0, q], south)
        S[q, zn, top] += RZ[0, q]
        send(("rz n", q), S.at[q, zn, top], ZC.at[0, q, top], north)
        take(("rz far s", q), RZ.at[1, q], north)
        S[q, zs, bottom] += RZ[1, q]
        send(("rz s", q), S.at[q, zs, bottom], ZC.at[1, q, bottom], south)
    for q in range(2):
        take(("rz now n", q), ZC.at[0, q, bottom], south)
        take(("rz now s", q), ZC.at[1, q, top], north)
        take(("rz n", q), ZC.at[0, q, top], south)
        take(("rz s", q), ZC.at[1, q, bottom], north)
        WI[zh, xx, q] = S[q, zh] + ZC[0, q] + ZC[1, q]

    w_away = describe(("turn w"), WI.at[zh, xx], WJ.at[col // 2, col % 2, u], mirror)
    x_away = describe(("turn x"), XJ.at[y, core, :, u], XI.at[row // NX, row % NX], mirror)
    w_stay = pltpu.make_async_copy(WI.at[zh, xx], WJ.at[y, core, u], lsem.at[2])
    x_stay = pltpu.make_async_copy(XJ.at[y, core, :, u], XI.at[zh, xx], lsem.at[3])

    @pl.when(jnp.logical_not(on_diagonal))
    def _():
        w_away.start()
        x_away.start()

    @pl.when(on_diagonal)
    def _():
        w_stay.start()
        x_stay.start()

    def lines():
        yield 7
        pl.when(jnp.logical_not(on_diagonal))(lambda: describe(("turn w"), WI.at[zh, xx], WJ.at[y, core, u], mirror).wait())
        pl.when(on_diagonal)(lambda: w_stay.wait())
        yield from gather_lines("W", WJ, 8, 2)

    def plane():
        yield 7.5
        pl.when(jnp.logical_not(on_diagonal))(
            lambda: describe(("turn x"), XJ.at[y, core, :, u], XI.at[zh, xx], mirror).wait()
        )
        pl.when(on_diagonal)(lambda: x_stay.wait())
        yield from gather_plane("XI", XI, 9, 3.5)

    run(gather_plane("WI", WI, 0, 3.5), lines(), plane())
    finish_plane("WI", WI)

    for q in range(2):
        WH[q], WL[q] = split(WJ[:, :, :, q].reshape(512, 512))
    finish_plane("XI", XI)

    scale = STEP_SIZE / (2.0 * count)
    limit = STEP_SIZE * PENALTY
    columns = lax.broadcasted_iota(jnp.int32, (NZ, 16, 512), 2)
    rows = lax.broadcasted_iota(jnp.int32, (NZ, 16, 512), 0) * (NX * 32) + lax.broadcasted_iota(jnp.int32, (NZ, 16, 512), 1)
    for by in (0, 1, -1, 2):
        at = ring(xx, by, NX)
        gram = jnp.zeros((NZ * 16, 512), F32)
        for q in range(2):
            gram += product(split(WI[:, at, q].reshape(NZ * 16, 512)), (XH[q], XL[q]), ((1,), (1,)))
            gram += product(split(XI[:, at, q].reshape(NZ * 16, 512)), (WH[q], WL[q]), ((1,), (1,)))
        old = OM[:, at]
        hit = jnp.logical_and(rows + (at * 32 + u * 16) == columns, on_diagonal)
        inverse = jnp.where(hit, STEP_SIZE / jnp.where(hit, old, 1.0), 0.0)
        moved = old - scale * gram.reshape(NZ, 16, 512) + inverse
        shrunk = (moved - jnp.minimum(jnp.maximum(moved, -limit), limit)) * SAME[:, at, u]
        out[:, at, u] = jnp.where(hit, moved, shrunk)
        send(("out", by), out.at[:, at, u], out.at[:, at, u], peer)
    for by in (0, 1, -1, 2):
        at = ring(xx, by, NX)
        take(("out", by), out.at[:, at, v], peer)
    for copy in sent:
        copy.wait_send()
    assert len(ids) <= SEMS


def shards(precision, residuals, labels):
    rows, samples = residuals.shape
    count = samples * lax.axis_size("smp")
    dma = pltpu.SemaphoreType.DMA
    any_space = pl.BlockSpec(memory_space=pl.ANY)
    vmem = pl.BlockSpec(memory_space=pltpu.VMEM)
    out = pl.pallas_call(
        lambda *refs: kernel(count, *refs),
        out_shape=jax.ShapeDtypeStruct((NZ, NX, 2, 16, 512), F32),
        in_specs=[any_space, any_space, vmem],
        out_specs=vmem,
        scratch_shapes=[
            pltpu.VMEM((NY, 2, 2, 2, 16, 512), F32),
            pltpu.VMEM((NY, 2, 2, 2, 16, 512), F32),
            pltpu.VMEM((NZ, NX, 2, 16, 512), F32),
            pltpu.VMEM((NZ, NX, 2, 16, 512), F32),
            pltpu.VMEM((NZ, NX, 2, 16, 512), F32),
            pltpu.VMEM((2, 2, 2, 16, 512), F32),
            pltpu.VMEM((2, 2, NZ, 16, 512), F32),
            pltpu.VMEM((2, NZ, 16, 512), F32),
            pltpu.VMEM((2, 2, 8, 512), F32),
            pltpu.VMEM((2, 2, 16, 512), F32),
            pltpu.VMEM((NZ, NX, 16, 512), F32),
            pltpu.VMEM((NZ, NX, 2, 16, 512), F32),
            pltpu.VMEM((2, 512, 512), BF16),
            pltpu.VMEM((2, 512, 512), BF16),
            pltpu.VMEM((2, 512, 512), BF16),
            pltpu.VMEM((2, 512, 512), BF16),
            dma((SEMS,)),
            dma((SEMS,)),
            dma((4,)),
        ],
        compiler_params=pltpu.CompilerParams(collective_id=0, has_side_effects=True, vmem_limit_bytes=48 * 2**20),
    )(
        precision.reshape(NZ, NX, 2, 16, 512).reshape(NZ, NX, 2, 16, 512),
        residuals.reshape(2, 16, 512),
        labels.reshape(16, 1, 512),
    )
    return out.reshape(512, 512)


def solution(mesh):
    return jax.shard_map(
        shards,
        mesh=mesh,
        in_specs=(P("row", "col"), P(("col", "row"), "smp"), P()),
        out_specs=P("row", "col"),
        check_vma=False,
    )
```

```python
import heapq

import jax
import jax.numpy as jnp
from jax import lax
from jax.experimental import pallas as pl
from jax.experimental.pallas import tpu as pltpu
from jax.sharding import PartitionSpec as P

STEP_SIZE = 0.5
PENALTY = 0.04
NY, NX, NZ = 8, 4, 4
SEMS = 400
XI_TIMES = (-9.0, -8.0, 0.5, 1.5, 2.0, 5.0, 9.0)
WI_TIMES = (8.0, 8.2, 11.7, 12.0, 13.0, 16.0, 17.5)
MESH = pl.DeviceIdType.MESH
F32, BF16 = jnp.float32, jnp.bfloat16


def split(a):
    high = a.astype(BF16)
    return high, (a - high.astype(F32)).astype(BF16)


def product(a, b, dims):
    (ah, al), (bh, bl) = a, b

    def dot(p, q):
        return lax.dot_general(p, q, (dims, ((), ())), preferred_element_type=F32)

    return dot(ah, bh) + dot(ah, bl) + dot(al, bh)


def line_slot(row, col):
    dz = (col // NX - row // NX + NZ) % NZ
    dx = (col % NX - row % NX + NX) % NX
    pair = (2 - dz + NZ) % NZ
    odd = (dx // 2 + 1 - pair // 2) % 2
    return ((row // 2 + 2 * pair + odd) % NY) * 2 + dx % 2


def plane_slot(block, y, core):
    away = (y - block // 2 + NY) % NY
    pair = away // 2
    dz = (2 - pair + NZ) % NZ
    dx = ((away % 2 + 1 - pair // 2) % 2) * 2 + core
    return ((block // NX + dz) % NZ) * NX + (block % NX + dx) % NX


def kernel(count, om, x, lab, out, XJ, WJ, WI, XI, PT, RX, RC, S, RZ, ZC, OM, SAME, WC, XH, XL, WIH, WIL, XIH, XIL, LAB, ssem, rsem, lsem):
    row, col, u = lax.axis_index("row"), lax.axis_index("col"), lax.axis_index("smp")
    y, core = row // 2, row % 2
    zh, xx = col // NX, col % NX
    v = 1 - u

    def ring(at, by, size):
        return lax.rem(at + by + size, size)

    up, down = {"row": ring(y, 1, NY) * 2 + core}, {"row": ring(y, -1, NY) * 2 + core}
    mate = {"row": y * 2 + 1 - core}
    east, west = {"col": zh * NX + ring(xx, 1, NX)}, {"col": zh * NX + ring(xx, -1, NX)}
    north, south = {"col": ring(zh, 1, NZ) * NX + xx}, {"col": ring(zh, -1, NZ) * NX + xx}
    peer = {"smp": v}
    to_line = {"row": line_slot(row, col), "col": row}
    to_plane = {"row": col, "col": plane_slot(col, y, core)}
    on_diagonal = row == col

    ids = {}
    sent = []

    def describe(key, src, dst, to):
        t = ids.setdefault(key, len(ids))
        return pltpu.make_async_remote_copy(
            src_ref=src, dst_ref=dst, send_sem=ssem.at[t], recv_sem=rsem.at[t], device_id=to, device_id_type=MESH
        )

    def send(key, src, dst, to):
        copy = describe(key, src, dst, to)
        copy.start()
        sent.append(copy)

    def take(key, dst, to):
        assert key in ids
        describe(key, dst, dst, to).wait_recv()

    load_x = pltpu.make_async_copy(x, XJ.at[row, u], lsem.at[0])
    load_om = pltpu.make_async_copy(om, OM, lsem.at[1])
    load_x.start()
    load_om.start()
    load_lab = pltpu.make_async_copy(lab, LAB, lsem.at[2])
    load_lab.start()

    barrier = pltpu.get_barrier_semaphore()
    ends = [{"row": ring(y, by, NY) * 2 + core} for by in (4, 3, -3, 2, -2)]
    near = (to_line, to_plane, *ends, north, south, east, west, up, down, peer, mate)
    for other in near:
        pl.semaphore_signal(barrier, inc=1, device_id=other, device_id_type=MESH)
    pl.semaphore_wait(barrier, len(near))
    load_x.wait()

    def to_mate(name, k, key, block):
        t = ids.setdefault((name, "mate", key), len(ids))
        r = ids.setdefault((name, "mate", k), len(ids))
        copy = pltpu.make_async_remote_copy(
            src_ref=block, dst_ref=block, send_sem=ssem.at[t], recv_sem=rsem.at[r], device_id=mate, device_id_type=MESH
        )
        copy.start()
        sent.append(copy)

    def take_mate(name, k, B, blocks):
        whole = B.at[pl.ds(0, blocks)]
        pltpu.make_async_remote_copy(
            src_ref=whole, dst_ref=whole, send_sem=ssem.at[0], recv_sem=rsem.at[ids[(name, "mate", k)]],
            device_id=mate, device_id_type=MESH,
        ).wait_recv()

    def gather_lines(name, B, place, all_on_y, start, pace):
        last = NY // 2

        def block(by, half, part=None):
            at = B.at[place(ring(y, by, NY)), half]
            return at if part is None else at.at[part]

        own = block(0, u)
        send((name, "z own"), own, own, peer)
        for part in range(2):
            for verb, way in (("up", up), ("down", down)):
                send((name, verb, 1, 0, part), own.at[part], own.at[part], way)
        to_mate(name, 0, "own", own)
        yield start + pace * 0.9
        theirs = block(0, v)
        take((name, "z own"), theirs, peer)
        parts = 2 if all_on_y else 1
        for part in range(parts):
            for verb, way in (("up", up), ("down", down)):
                send((name, verb, 1, 1, part), theirs.at[part], theirs.at[part], way)
        to_mate(name, 0, "own v", theirs)
        late = []

        def settle():
            for k, by in late:
                piece = block(by, v, 1)
                take((name, "z", by), piece, peer)
                to_mate(name, k, ("z", by), piece)
            late.clear()

        units = [(0, 0), (0, 1), (1, 0), (1, 1)][: 2 + parts]
        for k in range(1, last):
            for n, (other, part) in enumerate(units):
                yield start + pace * (k + n * 0.2)
                for verb, way, back, by in (("up", up, down, -k), ("down", down, up, k)):
                    piece = block(by, v if other else u, part)
                    take((name, verb, k, other, part), piece, back)
                    onward = k < last - 1
                    if k == last - 1:
                        onward = (part == (verb == "down")) if all_on_y or not other else False
                    if onward:
                        send((name, verb, k + 1, other, part), piece, piece, way)
                    if not all_on_y and (other, part) == (0, 1):
                        send((name, "z", by), piece, piece, peer)
                    to_mate(name, k, (by, other, part), piece)
            settle()
            if not all_on_y:
                late.extend([(k, -k), (k, k)])
        for other in range(2 if all_on_y else 1):
            yield start + pace * (last + other * 0.3)
            for part, verb, back in ((0, "up", down), (1, "down", up)):
                piece = block(last, v if other else u, part)
                take((name, verb, last, other, part), piece, back)
                if not all_on_y:
                    send((name, "z far", part), piece, piece, peer)
                to_mate(name, last, (other, part), piece)
        if not all_on_y:
            settle()
            yield start + pace * (last + 0.8)
            for part in range(2):
                piece = block(last, v, part)
                take((name, "z far", part), piece, peer)
                to_mate(name, last, ("v", part), piece)

    def gather_plane(name, B, place, times):
        def block(z_by, x_by):
            return B.at[place(ring(zh, z_by, NZ) * NX + ring(xx, x_by, NX))]

        def spread(z_by):
            at = block(z_by, 0)
            for part in range(2):
                send((name, "east", z_by, part), at.at[part], at.at[part], east)
                send((name, "west", z_by, 1 - part), at.at[1 - part], at.at[1 - part], west)

        def pass_on(z_by):
            at = block(z_by, -1)
            take((name, "east", z_by, 0), at.at[0], west)
            send((name, "east 2", z_by), at.at[0], at.at[0], east)
            at = block(z_by, 1)
            take((name, "west", z_by, 1), at.at[1], east)
            send((name, "west 2", z_by), at.at[1], at.at[1], west)

        own = block(0, 0)
        for part in range(2):
            send((name, "north", part), own.at[part], own.at[part], north)
            send((name, "south", 1 - part), own.at[1 - part], own.at[1 - part], south)
        spread(0)
        yield times[0]
        at = block(-1, 0)
        take((name, "north", 0), at.at[0], south)
        send((name, "north 2"), at.at[0], at.at[0], north)
        at = block(1, 0)
        take((name, "south", 1), at.at[1], north)
        send((name, "south 2"), at.at[1], at.at[1], south)
        take((name, "north", 1), block(-1, 0).at[1], south)
        spread(-1)
        take((name, "south", 0), block(1, 0).at[0], north)
        spread(1)
        yield times[1]
        pass_on(0)
        yield times[2]
        far = block(2, 0)
        take((name, "north 2"), far.at[0], south)
        take((name, "south 2"), far.at[1], north)
        spread(2)
        yield times[3]
        pass_on(-1)
        yield times[4]
        pass_on(1)
        yield times[5]
        pass_on(2)
        yield times[6]
        for z_by in (0, -1, 1, 2):
            take((name, "east", z_by, 1), block(z_by, -1).at[1], west)
            take((name, "west", z_by, 0), block(z_by, 1).at[0], east)
            far = block(z_by, 2)
            take((name, "east 2", z_by), far.at[0], west)
            take((name, "west 2", z_by), far.at[1], east)

    def run(*phases):
        heap = [(-1.0, n, phase) for n, phase in enumerate(phases)]
        heapq.heapify(heap)
        while heap:
            _, n, phase = heapq.heappop(heap)
            when = next(phase, None)
            if when is not None:
                heapq.heappush(heap, (when, n, phase))

    def at_x(by, half):
        return XJ.at[ring(y, by, NY) * 2 + core, half]

    own = at_x(0, u)
    send(("X", "z", 0), own, own, peer)
    orders = (1, -1, 2, -2, 3, -3, 4)
    for by in orders:
        send(("X", by), own, own, {"row": ring(y, by, NY) * 2 + core})
    to_mate("X", 0, "own", own)
    load_lab.wait()
    classes = lax.broadcasted_iota(jnp.int32, (8, 512), 0)
    ones = (LAB[row] == classes).astype(BF16), (LAB[col] == classes).astype(BF16)
    same = lax.dot_general(ones[0], ones[1], (((0,), (0,)), ((), ())), preferred_element_type=F32)
    SAME[...] = same.reshape(SAME.shape)
    theirs = at_x(0, v)
    take(("X", "z", 0), theirs, peer)
    send("turn x", XJ.at[row, :, u], XI.at[row], to_plane)
    to_mate("X", 1, "own v", theirs)
    for by in orders:
        piece = at_x(-by, u)
        take(("X", by), piece, up)
        to_mate("X", 0, by, piece)
        send(("X", "z", by), piece, piece, peer)
    take_mate("X", 0, XJ, 4)

    load_om.wait()
    x_parts = split(XJ[:, u].reshape(512, 512))
    XH[u], XL[u] = x_parts[0].reshape(NZ, 128, 512), x_parts[1].reshape(NZ, 128, 512)
    x2 = ring(xx, 2, NX)
    xe, xw = ring(xx, 1, NX), ring(xx, -1, NX)
    z2 = ring(zh, 2, NZ)
    zn, zs = ring(zh, 1, NZ), ring(zh, -1, NZ)
    low, high = pl.ds(0, 2), pl.ds(2, 2)
    for q in range(2):
        om_parts = split(OM[:, :, q].reshape(256, 512))
        PT[:, :, q] = product(om_parts, x_parts, ((1,), (0,))).reshape(NZ, NX, 16, 512)
        send(("rs far e", q), PT.at[low, x2, q], RX.at[0, q], east)
        send(("rs far w", q), PT.at[high, x2, q], RX.at[1, q], west)
        send(("rs now e", q), PT.at[high, xe, q], RC.at[0, q, high], east)
        send(("rs now w", q), PT.at[low, xw, q], RC.at[1, q, low], west)
    for q in range(2):
        take(("rs far e", q), RX.at[0, q], west)
        PT[low, xe, q] += RX[0, q]
        send(("rs e", q), PT.at[low, xe, q], RC.at[0, q, low], east)
        take(("rs far w", q), RX.at[1, q], east)
        PT[high, xw, q] += RX[1, q]
        send(("rs w", q), PT.at[high, xw, q], RC.at[1, q, high], west)
    take("turn x", XI.at[line_slot(row, col)], to_line)
    plane_x = gather_plane("XI", XI, lambda at: line_slot(row, at), XI_TIMES)
    next(plane_x)
    top, bottom = pl.ds(0, 8), pl.ds(8, 8)
    for q in range(2):
        take(("rs now e", q), RC.at[0, q, high], west)
        take(("rs now w", q), RC.at[1, q, low], east)
        take(("rs e", q), RC.at[0, q, low], west)
        take(("rs w", q), RC.at[1, q, high], east)
        S[q] = PT[:, xx, q] + RC[0, q] + RC[1, q]
        send(("rz far n", q), S.at[q, z2, top], RZ.at[0, q], north)
        send(("rz far s", q), S.at[q, z2, bottom], RZ.at[1, q], south)
        send(("rz now n", q), S.at[q, zn, bottom], ZC.at[0, q, bottom], north)
        send(("rz now s", q), S.at[q, zs, top], ZC.at[1, q, top], south)
    next(plane_x)
    for by in orders:
        piece = at_x(-by, v)
        take(("X", "z", by), piece, peer)
        to_mate("X", 1, by, piece)
    for q in range(2):
        take(("rz far n", q), RZ.at[0, q], south)
        S[q, zn, top] += RZ[0, q]
        send(("rz n", q), S.at[q, zn, top], ZC.at[0, q, top], north)
        take(("rz far s", q), RZ.at[1, q], north)
        S[q, zs, bottom] += RZ[1, q]
        send(("rz s", q), S.at[q, zs, bottom], ZC.at[1, q, bottom], south)
    mine = line_slot(row, col)
    arrives = plane_slot(col, y, core)
    for q in range(2):
        take(("rz now n", q), ZC.at[0, q, bottom], south)
        take(("rz now s", q), ZC.at[1, q, top], north)
        take(("rz n", q), ZC.at[0, q, top], south)
        take(("rz s", q), ZC.at[1, q, bottom], north)
        WC[q] = S[q, zh] + ZC[0, q] + ZC[1, q]
        send(("turn w", q), WC.at[q], WJ.at[col, u, q], to_line)
    send("swap", WC.at[v], WI.at[col, u], peer)
    WI[col, u] = WC[u]

    def lines_w():
        yield 7.0
        for q in range(2):
            take(("turn w", q), WJ.at[arrives, u, q], to_plane)
        yield from gather_lines("W", WJ, lambda at: plane_slot(col, at, core), True, 8.0, 3.6)

    scale = STEP_SIZE / (2.0 * count)
    limit = STEP_SIZE * PENALTY
    first = ((y - col // 2 + NY) % NY) // 2
    back = 1 - 2 * (((y - col // 2 + NY) % NY) % 2)

    def group(n):
        pair = ring(first, (0, -1, 1, 2)[n] * back, 4)
        return ring(col // NX + (2 - pair + NZ) % NZ, 0, NZ)

    def finish_group(n):
        g = group(n)
        lanes = pl.ds(pl.multiple_of(g * 128, 128), 128)
        gram = jnp.zeros((256, 128), F32)
        for q in range(2):
            gram += product((WIH[q], WIL[q]), (XH[q, g], XL[q, g]), ((1,), (1,)))
            w_parts = split(WJ[pl.ds(g * NX, NX), q].reshape(128, 512))
            gram += product((XIH[q], XIL[q]), w_parts, ((1,), (1,)))
        old = OM[:, :, u, :, lanes]
        rows = (lax.broadcasted_iota(jnp.int32, (NZ * NX, 16, 128), 0) * 32 + u * 16).reshape(NZ, NX, 16, 128)
        rows = rows + lax.broadcasted_iota(jnp.int32, (NZ, NX, 16, 128), 2)
        columns = lax.broadcasted_iota(jnp.int32, (NZ, NX, 16, 128), 3) + g * 128
        hit = jnp.logical_and(rows == columns, on_diagonal)
        inverse = jnp.where(hit, STEP_SIZE / jnp.where(hit, old, 1.0), 0.0)
        moved = old - scale * gram.reshape(NZ, NX, 16, 128) + inverse
        shrunk = (moved - jnp.minimum(jnp.maximum(moved, -limit), limit)) * SAME[:, :, u, :, lanes]
        out[:, :, u, :, lanes] = jnp.where(hit, moved, shrunk)
        piece = out.at[:, :, u, :, lanes]
        send(("out", n), piece, piece, peer)

    def grams():
        yield 9.5
        for q in range(2):
            XIH[q], XIL[q] = split(XI[:, q].reshape(256, 512))
        take_mate("X", 1, XJ, 4)
        XH[v], XL[v] = [part.reshape(NZ, 128, 512) for part in split(XJ[:, v].reshape(512, 512))]
        yield 17.6
        for q in range(2):
            WIH[q], WIL[q] = split(WI[:, q].reshape(256, 512))
        take_mate("W", 0, WJ, 1)
        take_mate("W", 1, WJ, 2)
        finish_group(0)
        yield 8.0 + 3.6 * 2 + 3.0
        take_mate("W", 2, WJ, 2)
        finish_group(1)
        yield 8.0 + 3.6 * 3 + 3.0
        take_mate("W", 3, WJ, 2)
        finish_group(2)
        yield 8.0 + 3.6 * 4 + 3.0
        take_mate("W", 4, WJ, 1)
        finish_group(3)

    def plane_w():
        yield 3.5
        take("swap", WI.at[col, v], peer)
        yield from gather_plane("WI", WI, lambda at: at, WI_TIMES)

    run(plane_x, plane_w(), lines_w(), grams())
    for n in range(4):
        piece = out.at[:, :, v, :, pl.ds(pl.multiple_of(group(n) * 128, 128), 128)]
        take(("out", n), piece, peer)
    for copy in sent:
        copy.wait_send()
    assert len(ids) <= SEMS


def shards(precision, residuals, labels):
    count = residuals.shape[1] * lax.axis_size("smp")
    dma = pltpu.SemaphoreType.DMA
    far = lambda a: pltpu.with_memory_space_constraint(a, pltpu.HBM)
    hbm = pl.BlockSpec(memory_space=pltpu.HBM)
    vmem = pl.BlockSpec(memory_space=pltpu.VMEM)
    out = pl.pallas_call(
        lambda *refs: kernel(count, *refs),
        out_shape=jax.ShapeDtypeStruct((NZ, NX, 2, 16, 512), F32),
        in_specs=[hbm, hbm, hbm],
        out_specs=vmem,
        scratch_shapes=[
            pltpu.VMEM((16, 2, 2, 16, 512), F32),
            pltpu.VMEM((16, 2, 2, 16, 512), F32),
            pltpu.VMEM((16, 2, 16, 512), F32),
            pltpu.VMEM((16, 2, 16, 512), F32),
            pltpu.VMEM((NZ, NX, 2, 16, 512), F32),
            pltpu.VMEM((2, 2, 2, 16, 512), F32),
            pltpu.VMEM((2, 2, NZ, 16, 512), F32),
            pltpu.VMEM((2, NZ, 16, 512), F32),
            pltpu.VMEM((2, 2, 8, 512), F32),
            pltpu.VMEM((2, 2, 16, 512), F32),
            pltpu.VMEM((NZ, NX, 2, 16, 512), F32),
            pltpu.VMEM((NZ, NX, 2, 16, 512), F32),
            pltpu.VMEM((2, 16, 512), F32),
            pltpu.VMEM((2, NZ, 128, 512), BF16),
            pltpu.VMEM((2, NZ, 128, 512), BF16),
            pltpu.VMEM((2, 256, 512), BF16),
            pltpu.VMEM((2, 256, 512), BF16),
            pltpu.VMEM((2, 256, 512), BF16),
            pltpu.VMEM((2, 256, 512), BF16),
            pltpu.VMEM((16, 1, 512), jnp.int32),
            dma((SEMS,)),
            dma((SEMS,)),
            dma((4,)),
        ],
        compiler_params=pltpu.CompilerParams(collective_id=0, has_side_effects=True, vmem_limit_bytes=48 * 2**20),
    )(
        far(precision.reshape(NZ, NX, 2, 16, 512)),
        far(residuals.reshape(2, 16, 512)),
        far(labels.reshape(16, 1, 512)),
    )
    return out.reshape(512, 512)


def solution(mesh):
    return jax.shard_map(
        shards,
        mesh=mesh,
        in_specs=(P("row", "col"), P(("col", "row"), "smp"), P()),
        out_specs=P("row", "col"),
        check_vma=False,
    )
```

```python
import heapq

import jax
import jax.numpy as jnp
from jax import lax
from jax.experimental import pallas as pl
from jax.experimental.pallas import tpu as pltpu
from jax.sharding import PartitionSpec as P

STEP_SIZE = 0.5
PENALTY = 0.04
NY, NX, NZ = 8, 4, 4
SEMS = 400
XI_TIMES = (-1.0, 1.0, 4.5, 5.0, 5.5, 8.0, 12.0)
WI_TIMES = (8.0, 8.2, 11.7, 12.0, 13.0, 16.0, 17.5)
MESH = pl.DeviceIdType.MESH
F32, BF16 = jnp.float32, jnp.bfloat16


def split(a):
    high = a.astype(BF16)
    return high, (a - high.astype(F32)).astype(BF16)


def product(a, b, dims):
    (ah, al), (bh, bl) = a, b

    def dot(p, q):
        return lax.dot_general(p, q, (dims, ((), ())), preferred_element_type=F32)

    return dot(ah, bh) + dot(ah, bl) + dot(al, bh)


def line_slot(row, col):
    dz = (col // NX - row // NX + NZ) % NZ
    dx = (col % NX - row % NX + NX) % NX
    pair = (2 - dz + NZ) % NZ
    odd = (dx // 2 + 1 - pair // 2) % 2
    return ((row // 2 + 2 * pair + odd) % NY) * 2 + dx % 2


def plane_slot(block, y, core):
    away = (y - block // 2 + NY) % NY
    pair = away // 2
    dz = (2 - pair + NZ) % NZ
    dx = ((away % 2 + 1 - pair // 2) % 2) * 2 + core
    return ((block // NX + dz) % NZ) * NX + (block % NX + dx) % NX


def kernel(count, om, x, lab, out, XJ, WJ, WI, XI, PT, RX, RC, S, RZ, ZC, OM, SAME, WC, LEAD, XH, XL, WIH, WIL, XIH, XIL, LAB, ssem, rsem, lsem):
    row, col, u = lax.axis_index("row"), lax.axis_index("col"), lax.axis_index("smp")
    y, core = row // 2, row % 2
    zh, xx = col // NX, col % NX
    v = 1 - u

    def ring(at, by, size):
        return lax.rem(at + by + size, size)

    up, down = {"row": ring(y, 1, NY) * 2 + core}, {"row": ring(y, -1, NY) * 2 + core}
    mate = {"row": y * 2 + 1 - core}
    east, west = {"col": zh * NX + ring(xx, 1, NX)}, {"col": zh * NX + ring(xx, -1, NX)}
    north, south = {"col": ring(zh, 1, NZ) * NX + xx}, {"col": ring(zh, -1, NZ) * NX + xx}
    peer = {"smp": v}
    to_line = {"row": line_slot(row, col), "col": row}
    to_plane = {"row": col, "col": plane_slot(col, y, core)}
    on_diagonal = row == col

    ids = {}
    sent = []

    def describe(key, src, dst, to):
        t = ids.setdefault(key, len(ids))
        return pltpu.make_async_remote_copy(
            src_ref=src, dst_ref=dst, send_sem=ssem.at[t], recv_sem=rsem.at[t], device_id=to, device_id_type=MESH
        )

    def send(key, src, dst, to):
        copy = describe(key, src, dst, to)
        copy.start()
        sent.append(copy)

    def take(key, dst, to):
        assert key in ids
        describe(key, dst, dst, to).wait_recv()

    load_x = pltpu.make_async_copy(x, XJ.at[row, u], lsem.at[0])
    load_om = pltpu.make_async_copy(om, OM, lsem.at[1])
    load_x.start()
    load_om.start()
    load_lab = pltpu.make_async_copy(lab, LAB, lsem.at[2])
    load_lab.start()

    barrier = pltpu.get_barrier_semaphore()
    ends = [{"row": ring(y, by, NY) * 2 + core} for by in (4, 3, -3, 2, -2)]
    near = (to_line, to_plane, *ends, north, south, east, west, up, down, peer, mate)
    for other in near:
        pl.semaphore_signal(barrier, inc=1, device_id=other, device_id_type=MESH)
    pl.semaphore_wait(barrier, len(near))
    load_x.wait()

    def to_mate(name, k, key, block):
        t = ids.setdefault((name, "mate", key), len(ids))
        r = ids.setdefault((name, "mate", k), len(ids))
        copy = pltpu.make_async_remote_copy(
            src_ref=block, dst_ref=block, send_sem=ssem.at[t], recv_sem=rsem.at[r], device_id=mate, device_id_type=MESH
        )
        copy.start()
        sent.append(copy)

    def take_mate(name, k, B, blocks):
        whole = B.at[pl.ds(0, blocks)]
        pltpu.make_async_remote_copy(
            src_ref=whole, dst_ref=whole, send_sem=ssem.at[0], recv_sem=rsem.at[ids[(name, "mate", k)]],
            device_id=mate, device_id_type=MESH,
        ).wait_recv()

    def gather_lines(name, B, place, all_on_y, start, pace):
        last = NY // 2

        def block(by, half, part=None):
            at = B.at[place(ring(y, by, NY)), half]
            return at if part is None else at.at[part]

        own = block(0, u)
        send((name, "z own"), own, own, peer)
        for part in range(2):
            for verb, way in (("up", up), ("down", down)):
                send((name, verb, 1, 0, part), own.at[part], own.at[part], way)
        to_mate(name, 0, "own", own)
        yield start + pace * 0.9
        theirs = block(0, v)
        take((name, "z own"), theirs, peer)
        parts = 2 if all_on_y else 1
        for part in range(parts):
            for verb, way in (("up", up), ("down", down)):
                send((name, verb, 1, 1, part), theirs.at[part], theirs.at[part], way)
        to_mate(name, 0, "own v", theirs)
        late = []

        def settle():
            for k, by in late:
                piece = block(by, v, 1)
                take((name, "z", by), piece, peer)
                to_mate(name, k, ("z", by), piece)
            late.clear()

        units = [(0, 0), (0, 1), (1, 0), (1, 1)][: 2 + parts]
        for k in range(1, last):
            for n, (other, part) in enumerate(units):
                yield start + pace * (k + n * 0.2)
                for verb, way, back, by in (("up", up, down, -k), ("down", down, up, k)):
                    piece = block(by, v if other else u, part)
                    take((name, verb, k, other, part), piece, back)
                    onward = k < last - 1
                    if k == last - 1:
                        onward = (part == (verb == "down")) if all_on_y or not other else False
                    if onward:
                        send((name, verb, k + 1, other, part), piece, piece, way)
                    if not all_on_y and (other, part) == (0, 1):
                        send((name, "z", by), piece, piece, peer)
                    to_mate(name, k, (by, other, part), piece)
            settle()
            if not all_on_y:
                late.extend([(k, -k), (k, k)])
        for other in range(2 if all_on_y else 1):
            yield start + pace * (last + other * 0.3)
            for part, verb, back in ((0, "up", down), (1, "down", up)):
                piece = block(last, v if other else u, part)
                take((name, verb, last, other, part), piece, back)
                if not all_on_y:
                    send((name, "z far", part), piece, piece, peer)
                to_mate(name, last, (other, part), piece)
        if not all_on_y:
            settle()
            yield start + pace * (last + 0.8)
            for part in range(2):
                piece = block(last, v, part)
                take((name, "z far", part), piece, peer)
                to_mate(name, last, ("v", part), piece)

    def gather_plane(name, B, place, times):
        def block(z_by, x_by):
            return B.at[place(ring(zh, z_by, NZ) * NX + ring(xx, x_by, NX))]

        def spread(z_by):
            at = block(z_by, 0)
            for part in range(2):
                send((name, "east", z_by, part), at.at[part], at.at[part], east)
                send((name, "west", z_by, 1 - part), at.at[1 - part], at.at[1 - part], west)

        def pass_on(z_by):
            at = block(z_by, -1)
            take((name, "east", z_by, 0), at.at[0], west)
            send((name, "east 2", z_by), at.at[0], at.at[0], east)
            at = block(z_by, 1)
            take((name, "west", z_by, 1), at.at[1], east)
            send((name, "west 2", z_by), at.at[1], at.at[1], west)

        own = block(0, 0)
        for part in range(2):
            send((name, "north", part), own.at[part], own.at[part], north)
            send((name, "south", 1 - part), own.at[1 - part], own.at[1 - part], south)
        spread(0)
        yield times[0]
        at = block(-1, 0)
        take((name, "north", 0), at.at[0], south)
        send((name, "north 2"), at.at[0], at.at[0], north)
        at = block(1, 0)
        take((name, "south", 1), at.at[1], north)
        send((name, "south 2"), at.at[1], at.at[1], south)
        take((name, "north", 1), block(-1, 0).at[1], south)
        spread(-1)
        take((name, "south", 0), block(1, 0).at[0], north)
        spread(1)
        yield times[1]
        pass_on(0)
        yield times[2]
        far = block(2, 0)
        take((name, "north 2"), far.at[0], south)
        take((name, "south 2"), far.at[1], north)
        spread(2)
        yield times[3]
        pass_on(-1)
        yield times[4]
        pass_on(1)
        yield times[5]
        pass_on(2)
        yield times[6]
        for z_by in (0, -1, 1, 2):
            take((name, "east", z_by, 1), block(z_by, -1).at[1], west)
            take((name, "west", z_by, 0), block(z_by, 1).at[0], east)
            far = block(z_by, 2)
            take((name, "east 2", z_by), far.at[0], west)
            take((name, "west 2", z_by), far.at[1], east)

    def run(*phases):
        heap = [(-1.0, n, phase) for n, phase in enumerate(phases)]
        heapq.heapify(heap)
        while heap:
            _, n, phase = heapq.heappop(heap)
            when = next(phase, None)
            if when is not None:
                heapq.heappush(heap, (when, n, phase))

    def at_x(by, half):
        return XJ.at[ring(y, by, NY) * 2 + core, half]

    own = at_x(0, u)
    send(("X", "z", 0), own, own, peer)
    orders = (1, -1, 2, -2, 3, -3, 4)
    for by in orders:
        send(("X", by), own, own, {"row": ring(y, by, NY) * 2 + core})
    to_mate("X", 0, "own", own)
    load_lab.wait()
    classes = lax.broadcasted_iota(jnp.int32, (8, 512), 0)
    ones = (LAB[row] == classes).astype(BF16), (LAB[col] == classes).astype(BF16)
    same = lax.dot_general(ones[0], ones[1], (((0,), (0,)), ((), ())), preferred_element_type=F32)
    SAME[...] = same.reshape(SAME.shape)
    theirs = at_x(0, v)
    take(("X", "z", 0), theirs, peer)
    to_mate("X", 1, "own v", theirs)
    for by in orders:
        piece = at_x(-by, u)
        take(("X", by), piece, up)
        to_mate("X", 0, by, piece)
        send(("X", "z", by), piece, piece, peer)
    take_mate("X", 0, XJ, 4)
    send("turn x", XJ.at[row, :, u], XI.at[row], to_plane)

    load_om.wait()
    x_parts = split(XJ[:, u].reshape(512, 512))
    XH[u], XL[u] = x_parts[0].reshape(NZ, 128, 512), x_parts[1].reshape(NZ, 128, 512)
    x2 = ring(xx, 2, NX)
    xe, xw = ring(xx, 1, NX), ring(xx, -1, NX)
    z2 = ring(zh, 2, NZ)
    zn, zs = ring(zh, 1, NZ), ring(zh, -1, NZ)
    low, high = pl.ds(0, 2), pl.ds(2, 2)
    for q in range(2):
        om_parts = split(OM[:, :, q].reshape(256, 512))
        PT[:, :, q] = product(om_parts, x_parts, ((1,), (0,))).reshape(NZ, NX, 16, 512)
        send(("rs far e", q), PT.at[low, x2, q], RX.at[0, q], east)
        send(("rs far w", q), PT.at[high, x2, q], RX.at[1, q], west)
        send(("rs now e", q), PT.at[high, xe, q], RC.at[0, q, high], east)
        send(("rs now w", q), PT.at[low, xw, q], RC.at[1, q, low], west)
    for q in range(2):
        take(("rs far e", q), RX.at[0, q], west)
        PT[low, xe, q] += RX[0, q]
        send(("rs e", q), PT.at[low, xe, q], RC.at[0, q, low], east)
        take(("rs far w", q), RX.at[1, q], east)
        PT[high, xw, q] += RX[1, q]
        send(("rs w", q), PT.at[high, xw, q], RC.at[1, q, high], west)
    top, bottom = pl.ds(0, 8), pl.ds(8, 8)
    for q in range(2):
        take(("rs now e", q), RC.at[0, q, high], west)
        take(("rs now w", q), RC.at[1, q, low], east)
        take(("rs e", q), RC.at[0, q, low], west)
        take(("rs w", q), RC.at[1, q, high], east)
        S[q] = PT[:, xx, q] + RC[0, q] + RC[1, q]
        send(("rz far n", q), S.at[q, z2, top], RZ.at[0, q], north)
        send(("rz far s", q), S.at[q, z2, bottom], RZ.at[1, q], south)
        send(("rz now n", q), S.at[q, zn, bottom], ZC.at[0, q, bottom], north)
        send(("rz now s", q), S.at[q, zs, top], ZC.at[1, q, top], south)
    take("turn x", XI.at[line_slot(row, col)], to_line)
    plane_x = gather_plane("XI", XI, lambda at: line_slot(row, at), XI_TIMES)
    next(plane_x)
    for by in orders:
        piece = at_x(-by, v)
        take(("X", "z", by), piece, peer)
        to_mate("X", 1, by, piece)
    for q in range(2):
        take(("rz far n", q), RZ.at[0, q], south)
        S[q, zn, top] += RZ[0, q]
        send(("rz n", q), S.at[q, zn, top], ZC.at[0, q, top], north)
        take(("rz far s", q), RZ.at[1, q], north)
        S[q, zs, bottom] += RZ[1, q]
        send(("rz s", q), S.at[q, zs, bottom], ZC.at[1, q, bottom], south)
    mine = line_slot(row, col)
    arrives = plane_slot(col, y, core)
    for q in range(2):
        take(("rz now n", q), ZC.at[0, q, bottom], south)
        take(("rz now s", q), ZC.at[1, q, top], north)
        take(("rz n", q), ZC.at[0, q, top], south)
        take(("rz s", q), ZC.at[1, q, bottom], north)
        WC[q] = S[q, zh] + ZC[0, q] + ZC[1, q]
        send(("turn w", q), WC.at[q], WJ.at[col, u, q], to_line)
    send("swap", WC.at[v], WI.at[col, u], peer)
    WI[col, u] = WC[u]

    def lines_w():
        yield 7.0
        for q in range(2):
            take(("turn w", q), WJ.at[arrives, u, q], to_plane)
        yield from gather_lines("W", WJ, lambda at: plane_slot(col, at, core), True, 8.0, 3.6)

    scale = STEP_SIZE / (2.0 * count)
    limit = STEP_SIZE * PENALTY
    first = ((y - col // 2 + NY) % NY) // 2
    back = 1 - 2 * (((y - col // 2 + NY) % NY) % 2)

    def group(n):
        pair = ring(first, (0, -1, 1, 2)[n] * back, 4)
        return ring(col // NX + (2 - pair + NZ) % NZ, 0, NZ)

    def lead_group(n):
        g = group(n)
        gram = jnp.zeros((256, 128), F32)
        for q in range(2):
            gram += product((WIH[q], WIL[q]), (XH[q, g], XL[q, g]), ((1,), (1,)))
        LEAD[...] = gram

    def finish_group(n):
        g = group(n)
        lanes = pl.ds(pl.multiple_of(g * 128, 128), 128)
        gram = LEAD[...]
        for q in range(2):
            w_parts = split(WJ[pl.ds(g * NX, NX), q].reshape(128, 512))
            gram += product((XIH[q], XIL[q]), w_parts, ((1,), (1,)))
        old = OM[:, :, u, :, lanes]
        rows = (lax.broadcasted_iota(jnp.int32, (NZ * NX, 16, 128), 0) * 32 + u * 16).reshape(NZ, NX, 16, 128)
        rows = rows + lax.broadcasted_iota(jnp.int32, (NZ, NX, 16, 128), 2)
        columns = lax.broadcasted_iota(jnp.int32, (NZ, NX, 16, 128), 3) + g * 128
        hit = jnp.logical_and(rows == columns, on_diagonal)
        inverse = jnp.where(hit, STEP_SIZE / jnp.where(hit, old, 1.0), 0.0)
        moved = old - scale * gram.reshape(NZ, NX, 16, 128) + inverse
        shrunk = (moved - jnp.minimum(jnp.maximum(moved, -limit), limit)) * SAME[:, :, u, :, lanes]
        out[:, :, u, :, lanes] = jnp.where(hit, moved, shrunk)
        piece = out.at[:, :, u, :, lanes]
        send(("out", n), piece, piece, peer)

    def grams():
        yield 12.5
        for q in range(2):
            XIH[q], XIL[q] = split(XI[:, q].reshape(256, 512))
        take_mate("X", 1, XJ, 4)
        XH[v], XL[v] = [part.reshape(NZ, 128, 512) for part in split(XJ[:, v].reshape(512, 512))]
        yield 17.6
        for q in range(2):
            WIH[q], WIL[q] = split(WI[:, q].reshape(256, 512))
        lead_group(0)
        take_mate("W", 0, WJ, 1)
        take_mate("W", 1, WJ, 2)
        finish_group(0)
        lead_group(1)
        yield 8.0 + 3.6 * 2 + 3.0
        take_mate("W", 2, WJ, 2)
        finish_group(1)
        lead_group(2)
        yield 8.0 + 3.6 * 3 + 3.0
        take_mate("W", 3, WJ, 2)
        finish_group(2)
        lead_group(3)
        yield 8.0 + 3.6 * 4 + 3.0
        take_mate("W", 4, WJ, 1)
        finish_group(3)

    def plane_w():
        yield 3.5
        take("swap", WI.at[col, v], peer)
        yield from gather_plane("WI", WI, lambda at: at, WI_TIMES)

    run(plane_x, plane_w(), lines_w(), grams())
    for n in range(4):
        piece = out.at[:, :, v, :, pl.ds(pl.multiple_of(group(n) * 128, 128), 128)]
        take(("out", n), piece, peer)
    for copy in sent:
        copy.wait_send()
    assert len(ids) <= SEMS


def shards(precision, residuals, labels):
    count = residuals.shape[1] * lax.axis_size("smp")
    dma = pltpu.SemaphoreType.DMA
    far = lambda a: pltpu.with_memory_space_constraint(a, pltpu.HBM)
    hbm = pl.BlockSpec(memory_space=pltpu.HBM)
    vmem = pl.BlockSpec(memory_space=pltpu.VMEM)
    out = pl.pallas_call(
        lambda *refs: kernel(count, *refs),
        out_shape=jax.ShapeDtypeStruct((NZ, NX, 2, 16, 512), F32),
        in_specs=[hbm, hbm, hbm],
        out_specs=vmem,
        scratch_shapes=[
            pltpu.VMEM((16, 2, 2, 16, 512), F32),
            pltpu.VMEM((16, 2, 2, 16, 512), F32),
            pltpu.VMEM((16, 2, 16, 512), F32),
            pltpu.VMEM((16, 2, 16, 512), F32),
            pltpu.VMEM((NZ, NX, 2, 16, 512), F32),
            pltpu.VMEM((2, 2, 2, 16, 512), F32),
            pltpu.VMEM((2, 2, NZ, 16, 512), F32),
            pltpu.VMEM((2, NZ, 16, 512), F32),
            pltpu.VMEM((2, 2, 8, 512), F32),
            pltpu.VMEM((2, 2, 16, 512), F32),
            pltpu.VMEM((NZ, NX, 2, 16, 512), F32),
            pltpu.VMEM((NZ, NX, 2, 16, 512), F32),
            pltpu.VMEM((2, 16, 512), F32),
            pltpu.VMEM((256, 128), F32),
            pltpu.VMEM((2, NZ, 128, 512), BF16),
            pltpu.VMEM((2, NZ, 128, 512), BF16),
            pltpu.VMEM((2, 256, 512), BF16),
            pltpu.VMEM((2, 256, 512), BF16),
            pltpu.VMEM((2, 256, 512), BF16),
            pltpu.VMEM((2, 256, 512), BF16),
            pltpu.VMEM((16, 1, 512), jnp.int32),
            dma((SEMS,)),
            dma((SEMS,)),
            dma((4,)),
        ],
        compiler_params=pltpu.CompilerParams(collective_id=0, has_side_effects=True, vmem_limit_bytes=48 * 2**20),
    )(
        far(precision.reshape(NZ, NX, 2, 16, 512)),
        far(residuals.reshape(2, 16, 512)),
        far(labels.reshape(16, 1, 512)),
    )
    return out.reshape(512, 512)


def solution(mesh):
    return jax.shard_map(
        shards,
        mesh=mesh,
        in_specs=(P("row", "col"), P(("col", "row"), "smp"), P()),
        out_specs=P("row", "col"),
        check_vma=False,
    )
```
